32 devices in a mesh: seq: 8 (over y, x, core), fsdp: 4 (over z).
Axes of the slice: x: 2, y: 2, z: 4, core: 2. Of those that a mesh axis runs over, the one named last changes fastest.
Arguments:
- block_input: bfloat16 [4, 2048, 768], P('fsdp', 'seq'), may hold values from -24 to 24
- out_grad: bfloat16 [4, 2048, 768], P('fsdp', 'seq'), may hold values from -6 to 6
- params: float32 [3768320], P(('seq', 'fsdp')), may hold values from -8 to 8
- first_moment: float32 [3768320], P(('seq', 'fsdp')), may hold values from -3 to 3
- second_moment: float32 [3768320], P(('seq', 'fsdp')), may hold values from 0.01 to 1
Outputs:
- block_output: float32 [4, 2048, 768], P('fsdp', 'seq')
- input_grad: float32 [4, 2048, 768], P('fsdp', 'seq')
- param_grad: float32 [3768320], P(('seq', 'fsdp'))
- new_params: float32 [3768320], P(('seq', 'fsdp'))
- new_first: float32 [3768320], P(('seq', 'fsdp'))
- new_second: float32 [3768320], P(('seq', 'fsdp'))
The draws below stay inside these ranges and needn't reach their ends.
All inputs are finite; a program needn't handle non-finite values.
Results may differ from the reference program's by a relative error of at most 0.023.
Values may be sent and summed in bfloat16 or wider, within the bound.
A program may use at most 192 MiB of HBM per device.

```python
import math
import jax
import jax.numpy as jnp
from jax import lax

MODEL_WIDTH = 768
MIXER_HEADS = 24
HEAD_DIM = 64
STATE = 128
KERNEL = 4
BLOCK = 256
TOK_DEV = 256
INNER = 1536
CHANNELS = 1792
PROJ = 3352
RAW = 3765320
PARAMS = 3768320
LENGTH = 2048
SEQS = 4


flurry_forward = 9.0


def flurry_heading(key):
    direction_raw = jax.random.normal(jax.random.fold_in(key, 901), (MODEL_WIDTH,), jnp.float32)
    return direction_raw / jnp.sqrt(jnp.sum(direction_raw * direction_raw))


def draw_params(key, part):
    random_subkeys = jax.random.split(jax.random.fold_in(key, 11), 12)
    travel_heading = flurry_heading(key)
    main_cols = jax.random.normal(random_subkeys[0], (MODEL_WIDTH, PROJ - MIXER_HEADS), jnp.float32) / math.sqrt(MODEL_WIDTH)
    timestep_columns = jax.random.normal(random_subkeys[1], (MODEL_WIDTH, MIXER_HEADS), jnp.float32) / math.sqrt(MODEL_WIDTH) + flurry_forward * travel_heading[:, None] / math.sqrt(MODEL_WIDTH)
    in_weight = jnp.concatenate([main_cols, timestep_columns], 1)
    out_weight = jax.random.normal(random_subkeys[2], (INNER, MODEL_WIDTH), jnp.float32) / math.sqrt(INNER)
    conv_weight = 0.5 * jax.random.normal(random_subkeys[3], (KERNEL, CHANNELS), jnp.float32)
    conv_bias = jax.random.uniform(random_subkeys[4], (CHANNELS,), jnp.float32, -1.0, 1.0)
    gain_input = jax.random.uniform(random_subkeys[5], (MODEL_WIDTH,), jnp.float32, 0.6, 1.4)
    gain_gated = jax.random.uniform(random_subkeys[6], (INNER,), jnp.float32, 0.6, 1.4)
    dt_bias = jax.random.uniform(random_subkeys[7], (MIXER_HEADS,), jnp.float32, -7.5, -6.5)
    slow_flag = jax.random.randint(random_subkeys[8], (MIXER_HEADS,), 0, 2)
    slow_rate = jnp.exp(jax.random.uniform(random_subkeys[9], (MIXER_HEADS,), jnp.float32, math.log(0.1), math.log(0.18)))
    fast_rate = jnp.exp(jax.random.uniform(random_subkeys[10], (MIXER_HEADS,), jnp.float32, math.log(12.0), math.log(40.0)))
    decay_rates = jnp.where(slow_flag == 1, slow_rate, fast_rate)
    a_log = jnp.log(decay_rates)
    skip_gain = jax.random.uniform(random_subkeys[11], (MIXER_HEADS,), jnp.float32, 0.5, 1.5)
    padding = 0.02 * jax.random.normal(jax.random.fold_in(key, 32), (PARAMS - RAW,), jnp.float32)
    flat_vector = jnp.concatenate([in_weight.reshape(-1), out_weight.reshape(-1), conv_weight.reshape(-1), conv_bias, gain_input, gain_gated, dt_bias, a_log, skip_gain, padding], 0)
    return jnp.clip(flat_vector, -8.0, 8.0)


def draw_block_input(key, part):
    starting_rows = jnp.clip(jax.random.normal(jax.random.fold_in(key, 21), (SEQS, LENGTH, MODEL_WIDTH), jnp.float32), -6.0, 6.0)
    spots = jax.random.randint(jax.random.fold_in(key, 22), (SEQS, 2), 0, LENGTH)
    match_count = jnp.any(jnp.arange(LENGTH)[None, :, None] == spots[:, None, :], axis=-1)
    travel_heading = flurry_heading(key)
    flurry_rows = travel_heading[None, None, :] * math.sqrt(MODEL_WIDTH) + 0.3 * starting_rows
    every_row = jnp.where(match_count[:, :, None], flurry_rows, starting_rows)
    return jnp.clip(every_row, -24.0, 24.0).astype(jnp.bfloat16)


def shard_levels(own_key, dims, cuts, least, top_value):
    level, own = 1.0, jax.random.fold_in(own_key, 6)
    for axis_at, blocks in cuts:
        heights = jnp.exp(jax.random.uniform(jax.random.fold_in(own, axis_at), (blocks,), jnp.float32, least / len(cuts), top_value / len(cuts)))
        level = level * jnp.repeat(heights, dims[axis_at] // blocks).reshape([-1 if axis == axis_at else 1 for axis in range(len(dims))])
    return level


def bell_draw(key, shape, scale, reach, cuts=(), kind=jnp.bfloat16):
    result = jax.random.normal(key, shape, jnp.float32) * scale
    if len(cuts) > 0:
        result = shard_levels(key, shape, cuts, -0.22, 0.18) * result
    return jnp.clip(result, min=-reach, max=reach).astype(kind)


def setup_inputs(seed: int = 0) -> dict:
    seeds = jax.random.split(jax.random.key(seed), 6)
    block_input = draw_block_input(jax.random.fold_in(seeds[5], 71), 0)
    out_grad = bell_draw(seeds[1], (SEQS, LENGTH, MODEL_WIDTH), 1.0, 6.0, ((0, 4), (1, 8)))
    params = draw_params(jax.random.fold_in(seeds[5], 71), 0)
    first_moment = bell_draw(seeds[3], (PARAMS,), 0.5, 3.0, ((0, 32),), jnp.float32)
    second_moment = jnp.clip(jnp.exp(math.log(1.0) - 4.6051702 * jax.random.uniform(seeds[4], (PARAMS,), jnp.float32) ** shard_levels(seeds[4], (PARAMS,), ((0, 32),), -0.2, 0.2)), 0.01, 1.0)
    return dict(block_input=block_input, out_grad=out_grad, params=params, first_moment=first_moment, second_moment=second_moment)


norm_epsilon = 1e-05
beta_one = 0.9
beta_two = 0.999
learn_rate = 0.02
weight_decay = 0.01
adam_epsilon = 1e-08
adam_step = 2
highest = lax.Precision.HIGHEST

def unpack(flat_vector):
    lengths = [MODEL_WIDTH * PROJ, INNER * MODEL_WIDTH, KERNEL * CHANNELS, CHANNELS, MODEL_WIDTH, INNER, MIXER_HEADS, MIXER_HEADS, MIXER_HEADS]
    shapes = [(MODEL_WIDTH, PROJ), (INNER, MODEL_WIDTH), (KERNEL, CHANNELS), (CHANNELS,), (MODEL_WIDTH,), (INNER,), (MIXER_HEADS,), (MIXER_HEADS,), (MIXER_HEADS,)]
    pieces = []
    offset = 0
    for length_one, shape_one in zip(lengths, shapes):
        pieces.append(flat_vector[offset:offset + length_one].reshape(shape_one))
        offset = offset + length_one
    return pieces

def pack(gradients):
    parts_list = [gradient.reshape(-1) for gradient in gradients]
    parts_list.append(jnp.zeros((PARAMS - RAW,), jnp.float32))
    return jnp.concatenate(parts_list, 0)

def state_space(values, inputs_b, outputs_c, log_decay, steps_dt, state_in):
    blocks_count = values.shape[0] // BLOCK
    causal = jnp.arange(BLOCK)[:, None] >= jnp.arange(BLOCK)[None, :]
    triangle = causal.astype(jnp.float32)

    def advance(carry_state, block_data):
        block_x, block_b, block_c, block_la, block_dt = block_data
        cumulative = jnp.dot(triangle, block_la, precision=highest)
        spread = cumulative.T[:, :, None] - cumulative.T[:, None, :]
        decays = jnp.exp(jnp.where(causal[None], spread, -10000.0))
        scores = jnp.dot(block_c, block_b.T, precision=highest)
        weights = scores[None] * decays * block_dt.T[:, None, :]
        inside = jnp.einsum('hij,jhp->ihp', weights, block_x, precision=highest)
        carried = jnp.einsum('hpn,in->ihp', carry_state, block_c, precision=highest) * jnp.exp(cumulative)[:, :, None]
        final_log = cumulative[-1]
        tail_weight = jnp.exp(final_log[None, :] - cumulative) * block_dt
        fresh_state = jnp.einsum('jhp,jn->hpn', tail_weight[:, :, None] * block_x, block_b, precision=highest)
        return (carry_state * jnp.exp(final_log)[:, None, None] + fresh_state, inside + carried)
    blocks = (values.reshape(blocks_count, BLOCK, MIXER_HEADS, HEAD_DIM), inputs_b.reshape(blocks_count, BLOCK, STATE), outputs_c.reshape(blocks_count, BLOCK, STATE), log_decay.reshape(blocks_count, BLOCK, MIXER_HEADS), steps_dt.reshape(blocks_count, BLOCK, MIXER_HEADS))
    state_out, outputs = lax.scan(jax.checkpoint(advance), state_in, blocks)
    return (outputs.reshape(values.shape), state_out)

def silu_grad(pre_act):
    logistic = jax.nn.sigmoid(pre_act)
    return logistic * (1.0 + pre_act * (1.0 - logistic))

def adam_update(weights, gradient, first, second):
    first_new = beta_one * first + (1.0 - beta_one) * gradient
    second_new = beta_two * second + (1.0 - beta_two) * gradient * gradient
    corrected = first_new / (1.0 - beta_one ** adam_step)
    scaled = jnp.sqrt(second_new / (1.0 - beta_two ** adam_step))
    weights_new = weights - learn_rate * (corrected / (scaled + adam_epsilon) + weight_decay * weights)
    return (weights_new, first_new, second_new)

def one_sequence(tokens_in, cotangent, pieces):
    in_weight, out_weight = (pieces[0], pieces[1])
    conv_weight = pieces[2].astype(jnp.float32)
    conv_bias = pieces[3].astype(jnp.float32)
    gain_input = pieces[4].astype(jnp.float32)
    gain_gated = pieces[5].astype(jnp.float32)
    dt_bias = pieces[6].astype(jnp.float32)
    a_log = pieces[7].astype(jnp.float32)
    skip_gain = pieces[8].astype(jnp.float32)
    tokens_all = tokens_in.shape[0]
    residual = tokens_in.astype(jnp.float32)
    inv_rms = lax.rsqrt(lax.optimization_barrier(jnp.mean(residual * residual, axis=-1, keepdims=True)) + norm_epsilon)
    normed = (residual * inv_rms * gain_input).astype(jnp.bfloat16)
    projected = jnp.dot(normed, in_weight, preferred_element_type=jnp.float32).astype(jnp.bfloat16)
    gate_z = projected[:, :INNER].astype(jnp.float32)
    conv_in = projected[:, INNER:INNER + CHANNELS]
    dt_raw = projected[:, INNER + CHANNELS:].astype(jnp.float32)
    padded = jnp.concatenate([jnp.zeros((KERNEL - 1, CHANNELS), jnp.bfloat16), conv_in], 0).astype(jnp.float32)
    conv_out = jnp.zeros((tokens_all, CHANNELS), jnp.float32) + conv_bias[None, :]
    for tap_index in range(KERNEL):
        conv_out = conv_out + conv_weight[tap_index][None, :] * padded[tap_index:tap_index + tokens_all]
    activated = jax.nn.silu(conv_out).astype(jnp.bfloat16)
    act_float = activated.astype(jnp.float32)
    values = act_float[:, :INNER].reshape(tokens_all, MIXER_HEADS, HEAD_DIM)
    inputs_b = act_float[:, INNER:INNER + STATE]
    outputs_c = act_float[:, INNER + STATE:]
    pre_dt = dt_raw + dt_bias[None, :]
    steps_dt = jax.nn.softplus(pre_dt)
    a_rate = -jnp.exp(a_log)
    log_decay = steps_dt * a_rate[None, :]
    zero_state = jnp.zeros((MIXER_HEADS, HEAD_DIM, STATE), jnp.float32)
    (ssd_out, state_end), pull_back = jax.vjp(state_space, values, inputs_b, outputs_c, log_decay, steps_dt, zero_state)
    mixed = (ssd_out + skip_gain[None, :, None] * values).reshape(tokens_all, INNER)
    gate_act = jax.nn.silu(gate_z)
    gated = mixed * gate_act
    inv_gated = lax.rsqrt(lax.optimization_barrier(jnp.mean(gated * gated, axis=-1, keepdims=True)) + norm_epsilon)
    normed_out = (gated * inv_gated * gain_gated).astype(jnp.bfloat16)
    output = residual + jnp.dot(normed_out, out_weight, preferred_element_type=jnp.float32)
    d_normed_out = jnp.dot(cotangent, out_weight.T, preferred_element_type=jnp.float32)
    gated_rows = d_normed_out * gated * inv_gated
    scaled_grad = d_normed_out * gain_gated
    d_gated = inv_gated * scaled_grad - gated * inv_gated ** 3 * lax.optimization_barrier(jnp.mean(scaled_grad * gated, axis=-1, keepdims=True))
    d_mixed = d_gated * gate_act
    d_gate_z = d_gated * mixed * silu_grad(gate_z)
    d_heads = d_mixed.reshape(tokens_all, MIXER_HEADS, HEAD_DIM)
    skip_rows = lax.optimization_barrier(jnp.sum(d_heads * values, 2))
    d_values, d_inputs_b, d_outputs_c, d_log_decay, d_steps, d_unused = pull_back((d_heads, jnp.zeros_like(state_end)))
    d_values = d_values + skip_gain[None, :, None] * d_heads
    d_steps = d_steps + d_log_decay * a_rate[None, :]
    alog_rows = d_log_decay * steps_dt
    d_pre_dt = d_steps * jax.nn.sigmoid(pre_dt)
    d_activated = jnp.concatenate([d_values.reshape(tokens_all, INNER), d_inputs_b, d_outputs_c], 1)
    d_conv_out = d_activated * silu_grad(conv_out)
    d_padded = jnp.zeros((tokens_all + KERNEL - 1, CHANNELS), jnp.float32)
    for tap_index in range(KERNEL):
        d_padded = d_padded + jnp.pad(d_conv_out * conv_weight[tap_index][None, :], ((tap_index, KERNEL - 1 - tap_index), (0, 0)))
    d_conv_in = d_padded[KERNEL - 1:]
    d_projected = jnp.concatenate([d_gate_z, d_conv_in, d_pre_dt], 1).astype(jnp.bfloat16)
    d_normed = jnp.dot(d_projected, in_weight.T, preferred_element_type=jnp.float32)
    input_rows = d_normed * residual * inv_rms
    scaled_in = d_normed * gain_input
    d_residual = inv_rms * scaled_in - residual * inv_rms ** 3 * lax.optimization_barrier(jnp.mean(scaled_in * residual, axis=-1, keepdims=True))
    input_grad = cotangent.astype(jnp.float32) + d_residual

    def piece_sum(running, index):
        start = index * TOK_DEV

        def rows(array):
            return lax.dynamic_slice_in_dim(array, start, TOK_DEV, 0)
        conv_rows = rows(d_conv_out)
        d_in_weight = jnp.dot(rows(normed).T, rows(d_projected), preferred_element_type=jnp.float32)
        d_out_weight = jnp.dot(rows(normed_out).T, rows(cotangent), preferred_element_type=jnp.float32)
        d_conv_weight = jnp.stack([lax.optimization_barrier(jnp.sum(conv_rows * lax.dynamic_slice_in_dim(padded, start + tap_index, TOK_DEV, 0), 0)) for tap_index in range(KERNEL)], 0)
        d_conv_bias = lax.optimization_barrier(jnp.sum(conv_rows, 0))
        d_gain_input = lax.optimization_barrier(jnp.sum(rows(input_rows), 0))
        d_gain_gated = lax.optimization_barrier(jnp.sum(rows(gated_rows), 0))
        d_dt_bias = lax.optimization_barrier(jnp.sum(rows(d_pre_dt), 0))
        d_a_log = lax.optimization_barrier(jnp.sum(rows(alog_rows), 0)) * a_rate
        d_skip = lax.optimization_barrier(jnp.sum(rows(skip_rows), 0))
        flat_piece = pack([d_in_weight, d_out_weight, d_conv_weight, d_conv_bias, d_gain_input, d_gain_gated, d_dt_bias, d_a_log, d_skip])
        rounded = lax.optimization_barrier(flat_piece.astype(jnp.bfloat16)).astype(jnp.float32)
        return (running + rounded, None)
    piece_ids = jnp.arange(tokens_all // TOK_DEV, dtype=jnp.int32)
    flat_grad, unused = lax.scan(piece_sum, jnp.zeros((PARAMS,), jnp.float32), piece_ids)
    return (output, input_grad, flat_grad)

def reference(block_input, out_grad, params, first_moment, second_moment):
    pieces = unpack(params.astype(jnp.bfloat16))

    def visit(running, pair_data):
        output, input_grad, flat_grad = one_sequence(pair_data[0], pair_data[1], pieces)
        return (running + flat_grad, (output, input_grad))
    total_grad, (outputs, input_grads) = lax.scan(visit, jnp.zeros((PARAMS,), jnp.float32), (block_input, out_grad))
    new_params, new_first, new_second = adam_update(params, total_grad, first_moment, second_moment)
    return (outputs, input_grads, total_grad, new_params, new_first, new_second)
```

```python
import itertools

import jax
import jax.numpy as jnp
from jax import lax
from jax.experimental import pallas as pl
from jax.experimental.pallas import tpu as pltpu
from jax.sharding import PartitionSpec as P

MODEL_WIDTH = 768
MIXER_HEADS = 24
HEAD_DIM = 64
STATE = 128
KERNEL = 4
BLOCK = 256
INNER = 1536
CHANNELS = 1792
PROJ = 3352
RAW = 3765320
PARAMS = 3768320


norm_epsilon = 1e-05
beta_one = 0.9
beta_two = 0.999
learn_rate = 0.02
weight_decay = 0.01
adam_epsilon = 1e-08
adam_step = 2
highest = lax.Precision.HIGHEST


def passed_along(value, axis, by):
    length = lax.axis_size(axis)
    pairs = [(i, i + by) for i in range(length) if 0 <= i + by < length]
    return lax.ppermute(value, axis, pairs)

def silu_grad(pre_act):
    logistic = jax.nn.sigmoid(pre_act)
    return logistic * (1.0 + pre_act * (1.0 - logistic))


def adam_update(weights, gradient, first, second):
    first_new = beta_one * first + (1.0 - beta_one) * gradient
    second_new = beta_two * second + (1.0 - beta_two) * gradient * gradient
    corrected = first_new / (1.0 - beta_one**adam_step)
    scaled = jnp.sqrt(second_new / (1.0 - beta_two**adam_step))
    weights_new = weights - learn_rate * (
        corrected / (scaled + adam_epsilon) + weight_decay * weights
    )
    return (weights_new, first_new, second_new)


LANES = 128
PAIR = 2 * HEAD_DIM
f32 = jnp.float32
bf16 = jnp.bfloat16


def dot_ab(a, b):
    return lax.dot_general(a, b, (((1,), (0,)), ((), ())), preferred_element_type=f32)


def dot_abt(a, b):
    return lax.dot_general(a, b, (((1,), (1,)), ((), ())), preferred_element_type=f32)


def dot_atb(a, b):
    return lax.dot_general(a, b, (((0,), (0,)), ((), ())), preferred_element_type=f32)


def column_of(array, index):
    lane = lax.broadcasted_iota(jnp.int32, array.shape, 1)
    return jnp.sum(jnp.where(lane == index, array, 0.0), axis=1, keepdims=True)


def masked_scores(b_ref, c_ref):
    scores = dot_abt(c_ref[...], b_ref[...])
    row = lax.broadcasted_iota(jnp.int32, scores.shape, 0)
    col = lax.broadcasted_iota(jnp.int32, scores.shape, 1)
    return jnp.where(row >= col, scores, 0.0), row >= col


def inside_kernel(x_ref, b_ref, c_ref, cum_ref, cum_t_ref, dt_t_ref, y_ref, score_ref):
    score_ref[...], _ = masked_scores(b_ref, c_ref)

    def one(pair, carry):
        lanes = pl.ds(pl.multiple_of(pair * PAIR, PAIR), PAIR)
        block = x_ref[:, lanes]
        halves = []
        for side in range(2):
            head = 2 * pair + side
            spread = column_of(cum_ref[...], head) - cum_t_ref[pl.ds(head, 1), :]
            decay = jnp.exp(jnp.minimum(spread, 0.0))
            weights = score_ref[...] * decay * dt_t_ref[pl.ds(head, 1), :]
            halves.append(dot_ab(weights.astype(bf16), block))
        lane = lax.broadcasted_iota(jnp.int32, halves[0].shape, 1)
        y_ref[:, lanes] = jnp.where(lane < HEAD_DIM, halves[0], halves[1])
        return carry

    lax.fori_loop(0, MIXER_HEADS // 2, one, 0)


def inside_grad_kernel(
    x_ref, dy_ref, b_ref, c_ref, cum_ref, cum_t_ref, dt_t_ref,
    dx_ref, db_ref, dc_ref, rows_ref, cols_ref, score_ref, dscore_ref,
):
    score_ref[...], causal = masked_scores(b_ref, c_ref)
    dscore_ref[...] = jnp.zeros_like(dscore_ref)
    rows_ref[...] = jnp.zeros_like(rows_ref)
    row_lane = lax.broadcasted_iota(jnp.int32, rows_ref.shape, 1)

    def one(pair, carry):
        lanes = pl.ds(pl.multiple_of(pair * PAIR, PAIR), PAIR)
        block = x_ref[:, lanes]
        dy = dy_ref[:, lanes]
        lane = lax.broadcasted_iota(jnp.int32, dy.shape, 1)
        halves = []
        for side in range(2):
            head = 2 * pair + side
            mine = (lane < HEAD_DIM) if side == 0 else (lane >= HEAD_DIM)
            dy_head = jnp.where(mine, dy, jnp.zeros_like(dy))
            dt_row = dt_t_ref[pl.ds(head, 1), :]
            spread = column_of(cum_ref[...], head) - cum_t_ref[pl.ds(head, 1), :]
            decay = jnp.exp(jnp.minimum(spread, 0.0))
            scaled = score_ref[...] * decay
            d_weights = dot_abt(dy_head, block)
            halves.append(dot_atb((scaled * dt_row).astype(bf16), dy_head))
            dscore_ref[...] += d_weights * decay * dt_row
            mass = d_weights * scaled
            cols_ref[pl.ds(head, 1), :] = jnp.sum(mass, axis=0, keepdims=True)
            row_sum = jnp.sum(mass * dt_row, axis=1, keepdims=True)
            rows_ref[...] += jnp.where(row_lane == head, row_sum, 0.0)
        dx_ref[:, lanes] = halves[0] + halves[1]
        return carry

    lax.fori_loop(0, MIXER_HEADS // 2, one, 0)
    d_scores = jnp.where(causal, dscore_ref[...], 0.0).astype(bf16)
    dc_ref[...] = dot_ab(d_scores, b_ref[...])
    db_ref[...] = dot_atb(d_scores, c_ref[...])


def whole_vmem(count):
    return [pl.BlockSpec(memory_space=pltpu.VMEM)] * count


def inside_forward(x, b, c, cum, cum_t, dt_t):
    tokens = x.shape[0]
    return pl.pallas_call(
        inside_kernel,
        out_shape=jax.ShapeDtypeStruct((tokens, INNER), f32),
        in_specs=whole_vmem(6),
        out_specs=pl.BlockSpec(memory_space=pltpu.VMEM),
        scratch_shapes=[pltpu.VMEM((tokens, tokens), f32)],
        cost_estimate=pl.CostEstimate(
            flops=4 * tokens * tokens * INNER, bytes_accessed=4 * tokens * INNER,
            transcendentals=tokens * tokens * MIXER_HEADS,
        ),
        name="inside_forward",
    )(x, b, c, cum, cum_t, dt_t)


def inside_backward(x, dy, b, c, cum, cum_t, dt_t):
    tokens = x.shape[0]
    return pl.pallas_call(
        inside_grad_kernel,
        out_shape=(
            jax.ShapeDtypeStruct((tokens, INNER), f32),
            jax.ShapeDtypeStruct((tokens, STATE), f32),
            jax.ShapeDtypeStruct((tokens, STATE), f32),
            jax.ShapeDtypeStruct((tokens, LANES), f32),
            jax.ShapeDtypeStruct((MIXER_HEADS, tokens), f32),
        ),
        in_specs=whole_vmem(7),
        out_specs=tuple(whole_vmem(5)),
        scratch_shapes=[pltpu.VMEM((tokens, tokens), f32), pltpu.VMEM((tokens, tokens), f32)],
        cost_estimate=pl.CostEstimate(
            flops=8 * tokens * tokens * INNER, bytes_accessed=8 * tokens * INNER,
            transcendentals=tokens * tokens * MIXER_HEADS,
        ),
        name="inside_backward",
    )(x, dy, b, c, cum, cum_t, dt_t)


def head_map():
    owner = lax.broadcasted_iota(jnp.int32, (MIXER_HEADS, INNER), 1) // HEAD_DIM
    return (owner == lax.broadcasted_iota(jnp.int32, (MIXER_HEADS, INNER), 0)).astype(f32)


def per_channel(value):
    return jnp.dot(value, head_map(), precision=highest)


def per_head(value):
    return lax.dot_general(
        value, head_map(), (((1,), (1,)), ((), ())), precision=highest, preferred_element_type=f32
    )


def bit_plan():
    seq_bits = lax.axis_size("seq").bit_length() - 1
    fsdp_bits = lax.axis_size("fsdp").bit_length() - 1
    dims = [("seq", bit) for bit in reversed(range(seq_bits))]
    dims += [("fsdp", bit) for bit in reversed(range(fsdp_bits))]
    middle = [("seq", bit) for bit in range(1, seq_bits)]
    last = [("fsdp", bit) for bit in range(fsdp_bits)]
    orders = [
        [dims.index(step) for step in [("seq", 0)] + middle + last],
        [dims.index(step) for step in [("seq", 0)] + middle[::-1] + last],
    ]
    return dims, orders


def kernels_fit(rows):
    seq, fsdp = lax.axis_size("seq"), lax.axis_size("fsdp")
    return rows % 8 == 0 and rows >= 64 and seq > 1 and seq & (seq - 1) == 0 and fsdp & (fsdp - 1) == 0


def row_streams(rows, parts):
    tiles = rows // 16
    edges = [16 * (tiles * part // parts) for part in range(parts)] + [rows]
    return list(zip(edges[:-1], edges[1:]))


def my_bits(dims):
    index = {axis: lax.axis_index(axis) for axis in ("seq", "fsdp")}
    return [(index[axis] // (1 << bit)) % 2 for axis, bit in dims], index


def partner_of(dims, index, bits, dim):
    axis, bit = dims[dim]
    return {axis: index[axis] + (1 - 2 * bits[dim]) * (1 << bit)}


def greet(dims, index, bits):
    barrier = pltpu.get_barrier_semaphore()
    for dim in range(len(dims)):
        pl.semaphore_signal(
            barrier, inc=1, device_id=partner_of(dims, index, bits, dim),
            device_id_type=pl.DeviceIdType.MESH,
        )
    pl.semaphore_wait(barrier, len(dims))


def scatter_sum(parts, rows):
    dims, orders = bit_plan()
    depth = len(dims)
    streams = row_streams(rows, 4)
    blocks = lax.axis_size("seq") * lax.axis_size("fsdp")
    copies = []
    start = 0
    for which, part in enumerate(parts):
        row = 0
        while row < part.shape[0]:
            block, inner = divmod(start + row, rows)
            size = min(rows - inner, part.shape[0] - row)
            copies.append((which, row, block, inner, size))
            row += size
        start += part.shape[0]
    assert start == blocks * rows

    def kernel(*refs):
        sources = refs[: len(parts)]
        out_ref, work, local_sem, send_sem, recv_sem = refs[len(parts) : len(parts) + 5]
        landing = refs[len(parts) + 5 :]
        bits, index = my_bits(dims)
        local = []
        for at, (which, row, block, inner, size) in enumerate(copies):
            where = tuple((block >> (depth - 1 - dim)) % 2 for dim in range(depth))
            copy = pltpu.make_async_copy(
                sources[which].at[pl.ds(row, size)],
                work.at[where + (pl.ds(inner, size),)],
                local_sem.at[at],
            )
            copy.start()
            local.append(copy)
        greet(dims, index, bits)
        for copy in local:
            copy.wait()
        sent = []

        def region(stream, stage, flip):
            first, last = streams[stream]
            order = orders[stream % 2]
            where = [slice(None)] * depth
            for dim in order[:stage]:
                where[dim] = bits[dim]
            where[order[stage]] = 1 - bits[order[stage]] if flip else bits[order[stage]]
            return where, pl.ds(first, last - first)

        def take(stream, stage):
            sent[stage * len(streams) + stream].wait_recv()
            arrived = landing[stage * len(streams) + stream]
            where, lines = region(stream, stage, False)
            free = [dim for dim in range(depth) if isinstance(where[dim], slice)]
            for choice in itertools.product(range(2), repeat=len(free)):
                spot = list(where)
                for dim, value in zip(free, choice):
                    spot[dim] = value
                total = work[tuple(spot) + (lines,)].astype(f32) + arrived[choice].astype(f32)
                if stage == depth - 1:
                    out_ref[lines] = total.astype(bf16)
                else:
                    work[tuple(spot) + (lines,)] = total.astype(bf16)

        for stage in range(depth):
            for stream in range(len(streams)):
                if stage > 0:
                    take(stream, stage - 1)
                where, lines = region(stream, stage, True)
                slot = stage * len(streams) + stream
                copy = pltpu.make_async_remote_copy(
                    src_ref=work.at[tuple(where) + (lines,)],
                    dst_ref=landing[slot],
                    send_sem=send_sem.at[slot],
                    recv_sem=recv_sem.at[slot],
                    device_id=partner_of(dims, index, bits, orders[stream % 2][stage]),
                    device_id_type=pl.DeviceIdType.MESH,
                )
                copy.start()
                sent.append(copy)
        for stream in range(len(streams)):
            take(stream, depth - 1)
        for copy in sent:
            copy.wait_send()

    slots = depth * len(streams)
    buffers = [
        pltpu.VMEM((2,) * (depth - 1 - stage) + (last - first, LANES), bf16)
        for stage in range(depth)
        for first, last in streams
    ]
    return pl.pallas_call(
        kernel,
        out_shape=jax.ShapeDtypeStruct((rows, LANES), bf16),
        in_specs=[pl.BlockSpec(memory_space=pl.ANY)] * len(parts),
        out_specs=pl.BlockSpec(memory_space=pltpu.VMEM),
        scratch_shapes=[
            pltpu.VMEM((2,) * depth + (rows, LANES), bf16),
            pltpu.SemaphoreType.DMA((len(copies),)),
            pltpu.SemaphoreType.DMA((slots,)),
            pltpu.SemaphoreType.DMA((slots,)),
        ] + buffers,
        compiler_params=pltpu.CompilerParams(
            collective_id=0, has_side_effects=True, vmem_limit_bytes=40 * 2**20
        ),
        name="scatter_sum",
    )(*parts)


def gather_all(shard):
    dims, orders = bit_plan()
    orders = [order[::-1] for order in orders]
    depth = len(dims)
    rows = shard.shape[0]
    streams = row_streams(rows, 4)

    def kernel(shard_ref, out_ref, local_sem, send_sem, recv_sem):
        bits, index = my_bits(dims)
        own = pltpu.make_async_copy(shard_ref, out_ref.at[tuple(bits)], local_sem)
        own.start()
        greet(dims, index, bits)
        own.wait()
        sent = []
        for stage in range(depth):
            for stream, (first, last) in enumerate(streams):
                order = orders[stream % 2]
                if stage > 0:
                    sent[(stage - 1) * len(streams) + stream].wait_recv()
                where = list(bits)
                for dim in order[:stage]:
                    where[dim] = slice(None)
                area = out_ref.at[tuple(where) + (pl.ds(first, last - first),)]
                slot = stage * len(streams) + stream
                copy = pltpu.make_async_remote_copy(
                    src_ref=area,
                    dst_ref=area,
                    send_sem=send_sem.at[slot],
                    recv_sem=recv_sem.at[slot],
                    device_id=partner_of(dims, index, bits, order[stage]),
                    device_id_type=pl.DeviceIdType.MESH,
                )
                copy.start()
                sent.append(copy)
        for copy in sent[-len(streams) :]:
            copy.wait_recv()
        for copy in sent:
            copy.wait_send()

    slots = depth * len(streams)
    whole = pl.pallas_call(
        kernel,
        out_shape=jax.ShapeDtypeStruct((2,) * depth + (rows, LANES), bf16),
        in_specs=[pl.BlockSpec(memory_space=pltpu.VMEM)],
        out_specs=pl.BlockSpec(memory_space=pl.ANY),
        scratch_shapes=[
            pltpu.SemaphoreType.DMA,
            pltpu.SemaphoreType.DMA((slots,)),
            pltpu.SemaphoreType.DMA((slots,)),
        ],
        compiler_params=pltpu.CompilerParams(collective_id=1, has_side_effects=True),
        name="gather_all",
    )(shard)
    return whole.reshape(-1, LANES)


def body(block_input, out_grad, params, first_moment, second_moment):
    shard_half = params.astype(bf16).reshape(-1, LANES)
    if kernels_fit(shard_half.shape[0]):
        whole_half = gather_all(shard_half)
    else:
        whole_half = lax.all_gather(shard_half, ("seq", "fsdp"), axis=0, tiled=True)
    sizes = [MODEL_WIDTH * PROJ, INNER * MODEL_WIDTH, KERNEL * CHANNELS, CHANNELS, MODEL_WIDTH, INNER]
    pieces = []
    row = 0
    for size in sizes:
        pieces.append(whole_half[row : row + size // LANES])
        row = row + size // LANES
    in_weight = pieces[0].reshape(MODEL_WIDTH, PROJ)
    out_weight = pieces[1].reshape(INNER, MODEL_WIDTH)
    conv_weight = pieces[2].astype(f32).reshape(KERNEL, CHANNELS)
    conv_bias = pieces[3].astype(f32).reshape(-1)
    gain_input = pieces[4].astype(f32).reshape(-1)
    gain_gated = pieces[5].astype(f32).reshape(-1)
    small = whole_half[row : row + 1].astype(f32).reshape(-1)
    dt_bias = small[:MIXER_HEADS]
    a_log = small[MIXER_HEADS : 2 * MIXER_HEADS]
    skip_gain = small[2 * MIXER_HEADS : 3 * MIXER_HEADS]
    residual = block_input[0].astype(f32)
    cotangent = out_grad[0]
    tokens_dev = residual.shape[0]
    inv_rms = lax.rsqrt(jnp.mean(residual * residual, axis=-1, keepdims=True) + norm_epsilon)
    normed = (residual * inv_rms * gain_input).astype(bf16)
    projected = jnp.dot(normed, in_weight, preferred_element_type=f32).astype(bf16)
    gate_z = projected[:, :INNER].astype(f32)
    conv_in = projected[:, INNER : INNER + CHANNELS]
    dt_raw = projected[:, INNER + CHANNELS :].astype(f32)
    left_rows = passed_along(conv_in[tokens_dev - KERNEL + 1 :], "seq", 1)
    padded = jnp.concatenate([left_rows, conv_in], 0).astype(f32)
    conv_out = jnp.zeros((tokens_dev, CHANNELS), f32) + conv_bias[None, :]
    for tap_index in range(KERNEL):
        conv_out = (
            conv_out + conv_weight[tap_index][None, :] * padded[tap_index : tap_index + tokens_dev]
        )
    activated = jax.nn.silu(conv_out).astype(bf16)
    x_half = activated[:, :INNER]
    b_half = activated[:, INNER : INNER + STATE]
    c_half = activated[:, INNER + STATE :]
    values = x_half.astype(f32)
    pre_dt = dt_raw + dt_bias[None, :]
    steps_dt = jax.nn.softplus(pre_dt)
    a_rate = -jnp.exp(a_log)
    log_decay = steps_dt * a_rate[None, :]
    causal = jnp.arange(tokens_dev)[:, None] >= jnp.arange(tokens_dev)[None, :]
    triangle = causal.astype(f32)
    cumulative = jnp.dot(triangle, log_decay, precision=highest)
    segment_log = cumulative[-1]
    cum_t, dt_t = cumulative.T, steps_dt.T
    cum_wide = jnp.pad(cumulative, ((0, 0), (0, LANES - MIXER_HEADS)))
    to_end = jnp.exp(segment_log[None, :] - cumulative)
    from_start = jnp.exp(cumulative)
    tail_weight = per_channel(to_end * steps_dt)
    head_weight = per_channel(from_start)
    x_tail = (values * tail_weight).astype(bf16)
    local_state = dot_atb(x_tail, b_half).astype(bf16)
    log_high = lax.reduce_precision(segment_log, 8, 7)
    log_rows = jnp.concatenate(
        [log_high, segment_log - log_high, jnp.zeros((LANES - 2 * MIXER_HEADS,), f32)]
    )
    log_rows = jnp.pad(log_rows[None, :], ((0, 15), (0, 0))).astype(bf16)
    count, mine = lax.axis_size("seq"), lax.axis_index("seq")
    gathered = lax.all_gather(jnp.concatenate([local_state, log_rows], 0), "seq")
    y_inside = inside_forward(x_half, b_half, c_half, cum_wide, cum_t, dt_t)
    logs = gathered[:, INNER].astype(f32)
    logs = logs[:, :MIXER_HEADS] + logs[:, MIXER_HEADS : 2 * MIXER_HEADS]
    source = jnp.arange(count)
    between = (source[None, :] > source[:, None]) & (source[None, :] < mine)
    earlier = jnp.exp(jnp.sum(jnp.where(between[:, :, None], logs[None], 0.0), 1))
    earlier = per_channel(jnp.where(source[:, None] < mine, earlier, 0.0))
    between = (source[None, :] < source[:, None]) & (source[None, :] > mine)
    later = jnp.exp(jnp.sum(jnp.where(between[:, :, None], logs[None], 0.0), 1))
    later = per_channel(jnp.where(source[:, None] > mine, later, 0.0))
    state_in = jnp.sum(gathered[:, :INNER].astype(f32) * earlier[:, :, None], 0)
    state_half = state_in.astype(bf16)
    y_carried = dot_abt(c_half, state_half) * head_weight
    skip_wide = per_channel(skip_gain[None, :])
    mixed = y_inside + y_carried + skip_wide * values
    gate_act = jax.nn.silu(gate_z)
    gated = mixed * gate_act
    inv_gated = lax.rsqrt(jnp.mean(gated * gated, axis=-1, keepdims=True) + norm_epsilon)
    normed_out = (gated * inv_gated * gain_gated).astype(bf16)
    output = residual + jnp.dot(normed_out, out_weight, preferred_element_type=f32)
    d_out_weight = dot_atb(normed_out, cotangent).astype(bf16)
    d_normed_out = dot_abt(cotangent, out_weight)
    d_gain_gated = jnp.sum(d_normed_out * gated * inv_gated, 0)
    scaled_grad = d_normed_out * gain_gated
    d_gated = inv_gated * scaled_grad - gated * inv_gated**3 * jnp.mean(
        scaled_grad * gated, axis=-1, keepdims=True
    )
    d_mixed = d_gated * gate_act
    d_gate_z = d_gated * mixed * silu_grad(gate_z)
    d_skip = per_head(jnp.sum(d_mixed * values, 0)[None, :])[0]
    dy_half = d_mixed.astype(bf16)
    dy_head = (d_mixed * head_weight).astype(bf16)
    local_grad = dot_atb(dy_head, c_half).astype(bf16)
    gathered_grad = lax.all_gather(local_grad, "seq")
    dx_inside, db_inside, dc_inside, row_mass, col_mass = inside_backward(
        x_half, dy_half, b_half, c_half, cum_wide, cum_t, dt_t
    )
    later_grad = jnp.sum(gathered_grad.astype(f32) * later[:, :, None], 0)
    grad_half = later_grad.astype(bf16)
    bg = dot_abt(b_half, grad_half)
    d_values = dx_inside + tail_weight * bg + skip_wide * d_mixed
    d_inputs_b = db_inside + dot_ab(x_tail, grad_half)
    d_outputs_c = dc_inside + dot_ab(dy_head, state_half)
    tail_mass = per_head(values * bg) * to_end
    d_steps_ssd = col_mass.T + tail_mass
    state_mass = per_head(jnp.sum(later_grad * state_in, 1)[None, :])[0]
    d_cumulative = row_mass[:, :MIXER_HEADS] + per_head(d_mixed * y_carried) - steps_dt * d_steps_ssd
    d_last = jnp.sum(steps_dt * tail_mass, 0) + jnp.exp(segment_log) * state_mass
    d_log_decay = d_last[None, :] + lax.dot_general(
        triangle, d_cumulative, (((0,), (0,)), ((), ())), precision=highest
    )
    d_steps = d_steps_ssd + d_log_decay * a_rate[None, :]
    d_a_log = jnp.sum(d_log_decay * steps_dt, 0) * a_rate
    d_pre_dt = d_steps * jax.nn.sigmoid(pre_dt)
    d_dt_bias = jnp.sum(d_pre_dt, 0)
    d_activated = jnp.concatenate([d_values, d_inputs_b, d_outputs_c], 1)
    d_conv_out = d_activated * silu_grad(conv_out)
    d_conv_bias = jnp.sum(d_conv_out, 0)
    d_conv_weight = jnp.stack(
        [
            jnp.sum(d_conv_out * padded[tap_index : tap_index + tokens_dev], 0)
            for tap_index in range(KERNEL)
        ],
        0,
    )
    d_padded = jnp.zeros((tokens_dev + KERNEL - 1, CHANNELS), jnp.float32)
    for tap_index in range(KERNEL):
        d_padded = d_padded + jnp.pad(
            d_conv_out * conv_weight[tap_index][None, :],
            ((tap_index, KERNEL - 1 - tap_index), (0, 0)),
        )
    right_rows = passed_along(d_padded[: KERNEL - 1], "seq", -1)
    d_conv_in = d_padded[KERNEL - 1 :]
    d_conv_in = jnp.concatenate(
        [d_conv_in[: tokens_dev - KERNEL + 1], d_conv_in[tokens_dev - KERNEL + 1 :] + right_rows], 0
    )
    d_projected = jnp.concatenate([d_gate_z, d_conv_in, d_pre_dt], 1).astype(jnp.bfloat16)
    d_in_weight = jnp.dot(normed.T, d_projected, preferred_element_type=jnp.float32)
    d_normed = jnp.dot(d_projected, in_weight.T, preferred_element_type=jnp.float32)
    d_gain_input = jnp.sum(d_normed * residual * inv_rms, 0)
    scaled_in = d_normed * gain_input
    d_residual = inv_rms * scaled_in - residual * inv_rms**3 * jnp.mean(
        scaled_in * residual, axis=-1, keepdims=True
    )
    input_grad = cotangent.astype(jnp.float32) + d_residual
    tail_vector = jnp.concatenate(
        [d_dt_bias, d_a_log, d_skip, jnp.zeros((PARAMS - RAW,), f32)]
    )
    small_parts = [d_conv_weight, d_conv_bias, d_gain_input, d_gain_gated, tail_vector]
    small_rows = jnp.concatenate([part.astype(bf16).reshape(-1, LANES) for part in small_parts], 0)
    parts = [d_in_weight.astype(bf16).reshape(-1, LANES), d_out_weight.reshape(-1, LANES), small_rows]
    if kernels_fit(shard_half.shape[0]):
        grad_shard = scatter_sum(parts, shard_half.shape[0])
    else:
        flat_local = jnp.concatenate(parts, 0)
        grad_shard = lax.psum_scatter(flat_local, ("seq", "fsdp"), scatter_dimension=0, tiled=True)
    grad_shard = grad_shard.reshape(-1).astype(f32)
    new_params, new_first, new_second = adam_update(params, grad_shard, first_moment, second_moment)
    return (output[None], input_grad[None], grad_shard, new_params, new_first, new_second)


def solution(mesh):
    return jax.shard_map(
        body,
        mesh=mesh,
        in_specs=(
            P("fsdp", "seq", None),
            P("fsdp", "seq", None),
            P(("seq", "fsdp")),
            P(("seq", "fsdp")),
            P(("seq", "fsdp")),
        ),
        out_specs=(
            P("fsdp", "seq", None),
            P("fsdp", "seq", None),
            P(("seq", "fsdp")),
            P(("seq", "fsdp")),
            P(("seq", "fsdp")),
            P(("seq", "fsdp")),
        ),
        check_vma=False,
    )
```

```python
import itertools

import jax
import jax.numpy as jnp
from jax import lax
from jax.experimental import pallas as pl
from jax.experimental.layout import Layout, with_layout_constraint
from jax.experimental.pallas import tpu as pltpu
from jax.sharding import PartitionSpec as P

MODEL_WIDTH = 768
MIXER_HEADS = 24
HEAD_DIM = 64
STATE = 128
KERNEL = 4
BLOCK = 256
INNER = 1536
CHANNELS = 1792
PROJ = 3352
RAW = 3765320
PARAMS = 3768320


norm_epsilon = 1e-05
beta_one = 0.9
beta_two = 0.999
learn_rate = 0.02
weight_decay = 0.01
adam_epsilon = 1e-08
adam_step = 2
highest = lax.Precision.HIGHEST


def passed_along(value, axis, by):
    length = lax.axis_size(axis)
    pairs = [(i, i + by) for i in range(length) if 0 <= i + by < length]
    return lax.ppermute(value, axis, pairs)

def silu_grad(pre_act):
    logistic = jax.nn.sigmoid(pre_act)
    return logistic * (1.0 + pre_act * (1.0 - logistic))


def adam_update(weights, gradient, first, second):
    first_new = beta_one * first + (1.0 - beta_one) * gradient
    second_new = beta_two * second + (1.0 - beta_two) * gradient * gradient
    corrected = first_new / (1.0 - beta_one**adam_step)
    scaled = jnp.sqrt(second_new / (1.0 - beta_two**adam_step))
    weights_new = weights - learn_rate * (
        corrected / (scaled + adam_epsilon) + weight_decay * weights
    )
    return (weights_new, first_new, second_new)


LANES = 128
PAIR = 2 * HEAD_DIM
f32 = jnp.float32
bf16 = jnp.bfloat16


def dot_ab(a, b):
    return lax.dot_general(a, b, (((1,), (0,)), ((), ())), preferred_element_type=f32)


def dot_abt(a, b):
    return lax.dot_general(a, b, (((1,), (1,)), ((), ())), preferred_element_type=f32)


def dot_atb(a, b):
    return lax.dot_general(a, b, (((0,), (0,)), ((), ())), preferred_element_type=f32)


def column_of(array, index):
    lane = lax.broadcasted_iota(jnp.int32, array.shape, 1)
    return jnp.sum(jnp.where(lane == index, array, 0.0), axis=1, keepdims=True)


def masked_scores(b_ref, c_ref):
    scores = dot_abt(c_ref[...], b_ref[...])
    row = lax.broadcasted_iota(jnp.int32, scores.shape, 0)
    col = lax.broadcasted_iota(jnp.int32, scores.shape, 1)
    return jnp.where(row >= col, scores, 0.0), row >= col


def inside_kernel(x_ref, b_ref, c_ref, cum_ref, cum_t_ref, dt_t_ref, y_ref, score_ref):
    score_ref[...], _ = masked_scores(b_ref, c_ref)

    def one(pair, carry):
        lanes = pl.ds(pl.multiple_of(pair * PAIR, PAIR), PAIR)
        block = x_ref[:, lanes]
        halves = []
        for side in range(2):
            head = 2 * pair + side
            spread = column_of(cum_ref[...], head) - cum_t_ref[pl.ds(head, 1), :]
            decay = jnp.exp(jnp.minimum(spread, 0.0))
            weights = score_ref[...] * decay * dt_t_ref[pl.ds(head, 1), :]
            halves.append(dot_ab(weights.astype(bf16), block))
        lane = lax.broadcasted_iota(jnp.int32, halves[0].shape, 1)
        y_ref[:, lanes] = jnp.where(lane < HEAD_DIM, halves[0], halves[1])
        return carry

    lax.fori_loop(0, MIXER_HEADS // 2, one, 0)


def inside_grad_kernel(
    x_ref, dy_ref, b_ref, c_ref, cum_ref, cum_t_ref, dt_t_ref,
    dx_ref, db_ref, dc_ref, rows_ref, cols_ref, score_ref, dscore_ref,
):
    score_ref[...], causal = masked_scores(b_ref, c_ref)
    dscore_ref[...] = jnp.zeros_like(dscore_ref)
    rows_ref[...] = jnp.zeros_like(rows_ref)
    row_lane = lax.broadcasted_iota(jnp.int32, rows_ref.shape, 1)

    def one(pair, carry):
        lanes = pl.ds(pl.multiple_of(pair * PAIR, PAIR), PAIR)
        block = x_ref[:, lanes]
        dy = dy_ref[:, lanes]
        lane = lax.broadcasted_iota(jnp.int32, dy.shape, 1)
        halves = []
        for side in range(2):
            head = 2 * pair + side
            mine = (lane < HEAD_DIM) if side == 0 else (lane >= HEAD_DIM)
            dy_head = jnp.where(mine, dy, jnp.zeros_like(dy))
            dt_row = dt_t_ref[pl.ds(head, 1), :]
            spread = column_of(cum_ref[...], head) - cum_t_ref[pl.ds(head, 1), :]
            decay = jnp.exp(jnp.minimum(spread, 0.0))
            scaled = score_ref[...] * decay
            d_weights = dot_abt(dy_head, block)
            halves.append(dot_atb((scaled * dt_row).astype(bf16), dy_head))
            dscore_ref[...] += d_weights * decay * dt_row
            mass = d_weights * scaled
            cols_ref[pl.ds(head, 1), :] = jnp.sum(mass, axis=0, keepdims=True)
            row_sum = jnp.sum(mass * dt_row, axis=1, keepdims=True)
            rows_ref[...] += jnp.where(row_lane == head, row_sum, 0.0)
        dx_ref[:, lanes] = halves[0] + halves[1]
        return carry

    lax.fori_loop(0, MIXER_HEADS // 2, one, 0)
    d_scores = jnp.where(causal, dscore_ref[...], 0.0).astype(bf16)
    dc_ref[...] = dot_ab(d_scores, b_ref[...])
    db_ref[...] = dot_atb(d_scores, c_ref[...])


def whole_vmem(count):
    return [pl.BlockSpec(memory_space=pltpu.VMEM)] * count


def inside_forward(x, b, c, cum, cum_t, dt_t):
    tokens = x.shape[0]
    return pl.pallas_call(
        inside_kernel,
        out_shape=jax.ShapeDtypeStruct((tokens, INNER), f32),
        in_specs=whole_vmem(6),
        out_specs=pl.BlockSpec(memory_space=pltpu.VMEM),
        scratch_shapes=[pltpu.VMEM((tokens, tokens), f32)],
        cost_estimate=pl.CostEstimate(
            flops=4 * tokens * tokens * INNER, bytes_accessed=4 * tokens * INNER,
            transcendentals=tokens * tokens * MIXER_HEADS,
        ),
        name="inside_forward",
    )(x, b, c, cum, cum_t, dt_t)


def inside_backward(x, dy, b, c, cum, cum_t, dt_t):
    tokens = x.shape[0]
    return pl.pallas_call(
        inside_grad_kernel,
        out_shape=(
            jax.ShapeDtypeStruct((tokens, INNER), f32),
            jax.ShapeDtypeStruct((tokens, STATE), f32),
            jax.ShapeDtypeStruct((tokens, STATE), f32),
            jax.ShapeDtypeStruct((tokens, LANES), f32),
            jax.ShapeDtypeStruct((MIXER_HEADS, tokens), f32),
        ),
        in_specs=whole_vmem(7),
        out_specs=tuple(whole_vmem(5)),
        scratch_shapes=[pltpu.VMEM((tokens, tokens), f32), pltpu.VMEM((tokens, tokens), f32)],
        cost_estimate=pl.CostEstimate(
            flops=8 * tokens * tokens * INNER, bytes_accessed=8 * tokens * INNER,
            transcendentals=tokens * tokens * MIXER_HEADS,
        ),
        name="inside_backward",
    )(x, dy, b, c, cum, cum_t, dt_t)


def row_major(array):
    return with_layout_constraint(array, Layout(major_to_minor=(0, 1)))


def head_map():
    owner = lax.broadcasted_iota(jnp.int32, (MIXER_HEADS, INNER), 1) // HEAD_DIM
    return (owner == lax.broadcasted_iota(jnp.int32, (MIXER_HEADS, INNER), 0)).astype(f32)


def per_channel(value):
    return jnp.dot(value, head_map(), precision=highest)


def per_head(value):
    return lax.dot_general(
        value, head_map(), (((1,), (1,)), ((), ())), precision=highest, preferred_element_type=f32
    )


def bit_plan():
    seq_bits = lax.axis_size("seq").bit_length() - 1
    fsdp_bits = lax.axis_size("fsdp").bit_length() - 1
    dims = [("seq", bit) for bit in reversed(range(seq_bits))]
    dims += [("fsdp", bit) for bit in reversed(range(fsdp_bits))]
    middle = [("seq", bit) for bit in range(1, seq_bits)]
    last = [("fsdp", bit) for bit in range(fsdp_bits)]
    orders = [
        [dims.index(step) for step in [("seq", 0)] + middle + last],
        [dims.index(step) for step in [("seq", 0)] + middle[::-1] + last],
    ]
    return dims, orders


def kernels_fit(rows):
    seq, fsdp = lax.axis_size("seq"), lax.axis_size("fsdp")
    return rows % 8 == 0 and rows >= 64 and seq > 1 and seq & (seq - 1) == 0 and fsdp & (fsdp - 1) == 0


def row_streams(rows, parts):
    tiles = rows // 16
    edges = [16 * (tiles * part // parts) for part in range(parts)] + [rows]
    return list(zip(edges[:-1], edges[1:]))


def my_bits(dims):
    index = {axis: lax.axis_index(axis) for axis in ("seq", "fsdp")}
    return [(index[axis] // (1 << bit)) % 2 for axis, bit in dims], index


def partner_of(dims, index, bits, dim):
    axis, bit = dims[dim]
    return {axis: index[axis] + (1 - 2 * bits[dim]) * (1 << bit)}


def greet(dims, index, bits):
    barrier = pltpu.get_barrier_semaphore()
    for dim in range(len(dims)):
        pl.semaphore_signal(
            barrier, inc=1, device_id=partner_of(dims, index, bits, dim),
            device_id_type=pl.DeviceIdType.MESH,
        )
    pl.semaphore_wait(barrier, len(dims))


def scatter_sum(parts, rows):
    dims, orders = bit_plan()
    depth = len(dims)
    streams = row_streams(rows, 4)
    blocks = lax.axis_size("seq") * lax.axis_size("fsdp")
    copies = []
    start = 0
    for which, part in enumerate(parts):
        row = 0
        while row < part.shape[0]:
            block, inner = divmod(start + row, rows)
            size = min(rows - inner, part.shape[0] - row)
            copies.append((which, row, block, inner, size))
            row += size
        start += part.shape[0]
    assert start == blocks * rows

    def kernel(*refs):
        sources = refs[: len(parts)]
        out_ref, work, local_sem, send_sem, recv_sem = refs[len(parts) : len(parts) + 5]
        landing = refs[len(parts) + 5 :]
        bits, index = my_bits(dims)
        local = []
        for at, (which, row, block, inner, size) in enumerate(copies):
            where = tuple((block >> (depth - 1 - dim)) % 2 for dim in range(depth))
            copy = pltpu.make_async_copy(
                sources[which].at[pl.ds(row, size)],
                work.at[where + (pl.ds(inner, size),)],
                local_sem.at[at],
            )
            copy.start()
            local.append(copy)
        greet(dims, index, bits)
        for copy in local:
            copy.wait()
        sent = []

        def region(stream, stage, flip):
            first, last = streams[stream]
            order = orders[stream % 2]
            where = [slice(None)] * depth
            for dim in order[:stage]:
                where[dim] = bits[dim]
            where[order[stage]] = 1 - bits[order[stage]] if flip else bits[order[stage]]
            return where, pl.ds(first, last - first)

        def take(stream, stage):
            sent[stage * len(streams) + stream].wait_recv()
            arrived = landing[stage * len(streams) + stream]
            where, lines = region(stream, stage, False)
            free = [dim for dim in range(depth) if isinstance(where[dim], slice)]
            for choice in itertools.product(range(2), repeat=len(free)):
                spot = list(where)
                for dim, value in zip(free, choice):
                    spot[dim] = value
                total = work[tuple(spot) + (lines,)].astype(f32) + arrived[choice].astype(f32)
                if stage == depth - 1:
                    out_ref[lines] = total.astype(bf16)
                else:
                    work[tuple(spot) + (lines,)] = total.astype(bf16)

        for stage in range(depth):
            for stream in range(len(streams)):
                if stage > 0:
                    take(stream, stage - 1)
                where, lines = region(stream, stage, True)
                slot = stage * len(streams) + stream
                copy = pltpu.make_async_remote_copy(
                    src_ref=work.at[tuple(where) + (lines,)],
                    dst_ref=landing[slot],
                    send_sem=send_sem.at[slot],
                    recv_sem=recv_sem.at[slot],
                    device_id=partner_of(dims, index, bits, orders[stream % 2][stage]),
                    device_id_type=pl.DeviceIdType.MESH,
                )
                copy.start()
                sent.append(copy)
        for stream in range(len(streams)):
            take(stream, depth - 1)
        for copy in sent:
            copy.wait_send()

    slots = depth * len(streams)
    buffers = [
        pltpu.VMEM((2,) * (depth - 1 - stage) + (last - first, LANES), bf16)
        for stage in range(depth)
        for first, last in streams
    ]
    return pl.pallas_call(
        kernel,
        out_shape=jax.ShapeDtypeStruct((rows, LANES), bf16),
        in_specs=[pl.BlockSpec(memory_space=pl.ANY)] * len(parts),
        out_specs=pl.BlockSpec(memory_space=pltpu.VMEM),
        scratch_shapes=[
            pltpu.VMEM((2,) * depth + (rows, LANES), bf16),
            pltpu.SemaphoreType.DMA((len(copies),)),
            pltpu.SemaphoreType.DMA((slots,)),
            pltpu.SemaphoreType.DMA((slots,)),
        ] + buffers,
        compiler_params=pltpu.CompilerParams(
            collective_id=0, has_side_effects=True, vmem_limit_bytes=40 * 2**20
        ),
        name="scatter_sum",
    )(*parts)


def gather_all(shard):
    dims, orders = bit_plan()
    orders = [order[::-1] for order in orders]
    depth = len(dims)
    rows = shard.shape[0]
    streams = row_streams(rows, 4)

    def kernel(shard_ref, out_ref, local_sem, send_sem, recv_sem):
        bits, index = my_bits(dims)
        own = pltpu.make_async_copy(shard_ref, out_ref.at[tuple(bits)], local_sem)
        own.start()
        greet(dims, index, bits)
        own.wait()
        sent = []
        for stage in range(depth):
            for stream, (first, last) in enumerate(streams):
                order = orders[stream % 2]
                if stage > 0:
                    sent[(stage - 1) * len(streams) + stream].wait_recv()
                where = list(bits)
                for dim in order[:stage]:
                    where[dim] = slice(None)
                area = out_ref.at[tuple(where) + (pl.ds(first, last - first),)]
                slot = stage * len(streams) + stream
                copy = pltpu.make_async_remote_copy(
                    src_ref=area,
                    dst_ref=area,
                    send_sem=send_sem.at[slot],
                    recv_sem=recv_sem.at[slot],
                    device_id=partner_of(dims, index, bits, order[stage]),
                    device_id_type=pl.DeviceIdType.MESH,
                )
                copy.start()
                sent.append(copy)
        for copy in sent[-len(streams) :]:
            copy.wait_recv()
        for copy in sent:
            copy.wait_send()

    slots = depth * len(streams)
    whole = pl.pallas_call(
        kernel,
        out_shape=jax.ShapeDtypeStruct((2,) * depth + (rows, LANES), bf16),
        in_specs=[pl.BlockSpec(memory_space=pltpu.VMEM)],
        out_specs=pl.BlockSpec(memory_space=pl.ANY),
        scratch_shapes=[
            pltpu.SemaphoreType.DMA,
            pltpu.SemaphoreType.DMA((slots,)),
            pltpu.SemaphoreType.DMA((slots,)),
        ],
        compiler_params=pltpu.CompilerParams(collective_id=1, has_side_effects=True),
        name="gather_all",
    )(shard)
    return whole.reshape(-1, LANES)


def body(block_input, out_grad, params, first_moment, second_moment):
    shard_half = params.astype(bf16).reshape(-1, LANES)
    if kernels_fit(shard_half.shape[0]):
        whole_half = gather_all(shard_half)
    else:
        whole_half = lax.all_gather(shard_half, ("seq", "fsdp"), axis=0, tiled=True)
    sizes = [MODEL_WIDTH * PROJ, INNER * MODEL_WIDTH, KERNEL * CHANNELS, CHANNELS, MODEL_WIDTH, INNER]
    pieces = []
    row = 0
    for size in sizes:
        pieces.append(whole_half[row : row + size // LANES])
        row = row + size // LANES
    in_weight = pieces[0].reshape(MODEL_WIDTH, PROJ)
    out_weight = pieces[1].reshape(INNER, MODEL_WIDTH)
    conv_weight = pieces[2].astype(f32).reshape(KERNEL, CHANNELS)
    conv_bias = pieces[3].astype(f32).reshape(-1)
    gain_input = pieces[4].astype(f32).reshape(-1)
    gain_gated = pieces[5].astype(f32).reshape(-1)
    small = whole_half[row : row + 1].astype(f32).reshape(-1)
    dt_bias = small[:MIXER_HEADS]
    a_log = small[MIXER_HEADS : 2 * MIXER_HEADS]
    skip_gain = small[2 * MIXER_HEADS : 3 * MIXER_HEADS]
    residual = block_input[0].astype(f32)
    cotangent = out_grad[0]
    tokens_dev = residual.shape[0]
    inv_rms = lax.rsqrt(jnp.mean(residual * residual, axis=-1, keepdims=True) + norm_epsilon)
    normed = (residual * inv_rms * gain_input).astype(bf16)
    projected = row_major(jnp.dot(normed, in_weight, preferred_element_type=f32).astype(bf16))
    gate_z = projected[:, :INNER].astype(f32)
    conv_in = projected[:, INNER : INNER + CHANNELS]
    dt_raw = projected[:, INNER + CHANNELS :].astype(f32)
    left_rows = passed_along(conv_in[tokens_dev - KERNEL + 1 :], "seq", 1)
    padded = jnp.concatenate([left_rows, conv_in], 0).astype(f32)
    conv_out = jnp.zeros((tokens_dev, CHANNELS), f32) + conv_bias[None, :]
    for tap_index in range(KERNEL):
        conv_out = (
            conv_out + conv_weight[tap_index][None, :] * padded[tap_index : tap_index + tokens_dev]
        )
    activated = row_major(jax.nn.silu(conv_out).astype(bf16))
    x_half = activated[:, :INNER]
    b_half = activated[:, INNER : INNER + STATE]
    c_half = activated[:, INNER + STATE :]
    values = x_half.astype(f32)
    pre_dt = dt_raw + dt_bias[None, :]
    steps_dt = jax.nn.softplus(pre_dt)
    a_rate = -jnp.exp(a_log)
    log_decay = steps_dt * a_rate[None, :]
    causal = jnp.arange(tokens_dev)[:, None] >= jnp.arange(tokens_dev)[None, :]
    triangle = causal.astype(f32)
    cumulative = jnp.dot(triangle, log_decay, precision=highest)
    segment_log = cumulative[-1]
    cum_t, dt_t = cumulative.T, steps_dt.T
    cum_wide = jnp.pad(cumulative, ((0, 0), (0, LANES - MIXER_HEADS)))
    to_end = jnp.exp(segment_log[None, :] - cumulative)
    from_start = jnp.exp(cumulative)
    tail_weight = per_channel(to_end * steps_dt)
    head_weight = per_channel(from_start)
    x_tail = (values * tail_weight).astype(bf16)
    local_state = dot_atb(x_tail, b_half).astype(bf16)
    log_high = lax.reduce_precision(segment_log, 8, 7)
    log_rows = jnp.concatenate(
        [log_high, segment_log - log_high, jnp.zeros((LANES - 2 * MIXER_HEADS,), f32)]
    )
    log_rows = jnp.pad(log_rows[None, :], ((0, 15), (0, 0))).astype(bf16)
    count, mine = lax.axis_size("seq"), lax.axis_index("seq")
    gathered = lax.all_gather(jnp.concatenate([local_state, log_rows], 0), "seq")
    y_inside = inside_forward(x_half, b_half, c_half, cum_wide, cum_t, dt_t)
    logs = gathered[:, INNER].astype(f32)
    logs = logs[:, :MIXER_HEADS] + logs[:, MIXER_HEADS : 2 * MIXER_HEADS]
    source = jnp.arange(count)
    between = (source[None, :] > source[:, None]) & (source[None, :] < mine)
    earlier = jnp.exp(jnp.sum(jnp.where(between[:, :, None], logs[None], 0.0), 1))
    earlier = per_channel(jnp.where(source[:, None] < mine, earlier, 0.0))
    between = (source[None, :] < source[:, None]) & (source[None, :] > mine)
    later = jnp.exp(jnp.sum(jnp.where(between[:, :, None], logs[None], 0.0), 1))
    later = per_channel(jnp.where(source[:, None] > mine, later, 0.0))
    state_in = jnp.sum(gathered[:, :INNER].astype(f32) * earlier[:, :, None], 0)
    state_half = state_in.astype(bf16)
    y_carried = dot_abt(c_half, state_half) * head_weight
    skip_wide = per_channel(skip_gain[None, :])
    y_carried = row_major(y_carried)
    mixed = y_inside + y_carried + skip_wide * values
    gate_act = jax.nn.silu(gate_z)
    gated = mixed * gate_act
    inv_gated = lax.rsqrt(jnp.mean(gated * gated, axis=-1, keepdims=True) + norm_epsilon)
    normed_out = (gated * inv_gated * gain_gated).astype(bf16)
    output = residual + jnp.dot(normed_out, out_weight, preferred_element_type=f32)
    d_out_weight = dot_atb(normed_out, cotangent).astype(bf16)
    d_normed_out = row_major(dot_abt(cotangent, out_weight))
    d_gain_gated = jnp.sum(d_normed_out * gated * inv_gated, 0)
    scaled_grad = d_normed_out * gain_gated
    d_gated = inv_gated * scaled_grad - gated * inv_gated**3 * jnp.mean(
        scaled_grad * gated, axis=-1, keepdims=True
    )
    d_mixed = d_gated * gate_act
    d_gate_z = d_gated * mixed * silu_grad(gate_z)
    d_skip = per_head(jnp.sum(d_mixed * values, 0)[None, :])[0]
    dy_half = row_major(d_mixed.astype(bf16))
    dy_head = (d_mixed * head_weight).astype(bf16)
    local_grad = dot_atb(dy_head, c_half).astype(bf16)
    gathered_grad = lax.all_gather(local_grad, "seq")
    dx_inside, db_inside, dc_inside, row_mass, col_mass = inside_backward(
        x_half, dy_half, b_half, c_half, cum_wide, cum_t, dt_t
    )
    later_grad = jnp.sum(gathered_grad.astype(f32) * later[:, :, None], 0)
    grad_half = later_grad.astype(bf16)
    bg = row_major(dot_abt(b_half, grad_half))
    d_values = dx_inside + tail_weight * bg + skip_wide * d_mixed
    d_inputs_b = db_inside + dot_ab(x_tail, grad_half)
    d_outputs_c = dc_inside + dot_ab(dy_head, state_half)
    tail_mass = per_head(values * bg) * to_end
    d_steps_ssd = col_mass.T + tail_mass
    state_mass = per_head(jnp.sum(later_grad * state_in, 1)[None, :])[0]
    d_cumulative = row_mass[:, :MIXER_HEADS] + per_head(d_mixed * y_carried) - steps_dt * d_steps_ssd
    d_last = jnp.sum(steps_dt * tail_mass, 0) + jnp.exp(segment_log) * state_mass
    d_log_decay = d_last[None, :] + lax.dot_general(
        triangle, d_cumulative, (((0,), (0,)), ((), ())), precision=highest
    )
    d_steps = d_steps_ssd + d_log_decay * a_rate[None, :]
    d_a_log = jnp.sum(d_log_decay * steps_dt, 0) * a_rate
    d_pre_dt = d_steps * jax.nn.sigmoid(pre_dt)
    d_dt_bias = jnp.sum(d_pre_dt, 0)
    d_activated = jnp.concatenate([d_values, d_inputs_b, d_outputs_c], 1)
    d_conv_out = row_major(d_activated * silu_grad(conv_out))
    d_conv_bias = jnp.sum(d_conv_out, 0)
    d_conv_weight = jnp.stack(
        [
            jnp.sum(d_conv_out * padded[tap_index : tap_index + tokens_dev], 0)
            for tap_index in range(KERNEL)
        ],
        0,
    )
    d_padded = jnp.zeros((tokens_dev + KERNEL - 1, CHANNELS), jnp.float32)
    for tap_index in range(KERNEL):
        d_padded = d_padded + jnp.pad(
            d_conv_out * conv_weight[tap_index][None, :],
            ((tap_index, KERNEL - 1 - tap_index), (0, 0)),
        )
    right_rows = passed_along(d_padded[: KERNEL - 1], "seq", -1)
    d_conv_in = d_padded[KERNEL - 1 :]
    d_conv_in = jnp.concatenate(
        [d_conv_in[: tokens_dev - KERNEL + 1], d_conv_in[tokens_dev - KERNEL + 1 :] + right_rows], 0
    )
    d_projected = row_major(jnp.concatenate([d_gate_z, d_conv_in, d_pre_dt], 1).astype(bf16))
    d_in_weight = row_major(dot_atb(normed, d_projected).astype(bf16))
    d_normed = jnp.dot(d_projected, in_weight.T, preferred_element_type=jnp.float32)
    d_gain_input = jnp.sum(d_normed * residual * inv_rms, 0)
    scaled_in = d_normed * gain_input
    d_residual = inv_rms * scaled_in - residual * inv_rms**3 * jnp.mean(
        scaled_in * residual, axis=-1, keepdims=True
    )
    input_grad = cotangent.astype(jnp.float32) + d_residual
    tail_vector = jnp.concatenate(
        [d_dt_bias, d_a_log, d_skip, jnp.zeros((PARAMS - RAW,), f32)]
    )
    small_parts = [d_conv_weight, d_conv_bias, d_gain_input, d_gain_gated, tail_vector]
    small_rows = jnp.concatenate([part.astype(bf16).reshape(-1, LANES) for part in small_parts], 0)
    parts = [d_in_weight.astype(bf16).reshape(-1, LANES), d_out_weight.reshape(-1, LANES), small_rows]
    if kernels_fit(shard_half.shape[0]):
        grad_shard = scatter_sum(parts, shard_half.shape[0])
    else:
        flat_local = jnp.concatenate(parts, 0)
        grad_shard = lax.psum_scatter(flat_local, ("seq", "fsdp"), scatter_dimension=0, tiled=True)
    grad_shard = grad_shard.reshape(-1).astype(f32)
    new_params, new_first, new_second = adam_update(params, grad_shard, first_moment, second_moment)
    return (output[None], input_grad[None], grad_shard, new_params, new_first, new_second)


def solution(mesh):
    return jax.shard_map(
        body,
        mesh=mesh,
        in_specs=(
            P("fsdp", "seq", None),
            P("fsdp", "seq", None),
            P(("seq", "fsdp")),
            P(("seq", "fsdp")),
            P(("seq", "fsdp")),
        ),
        out_specs=(
            P("fsdp", "seq", None),
            P("fsdp", "seq", None),
            P(("seq", "fsdp")),
            P(("seq", "fsdp")),
            P(("seq", "fsdp")),
            P(("seq", "fsdp")),
        ),
        check_vma=False,
    )
```

```python
import itertools

import jax
import jax.numpy as jnp
from jax import lax
from jax.experimental import pallas as pl
from jax.experimental.layout import Layout, with_layout_constraint
from jax.experimental.pallas import tpu as pltpu
from jax.sharding import PartitionSpec as P

MODEL_WIDTH = 768
MIXER_HEADS = 24
HEAD_DIM = 64
STATE = 128
KERNEL = 4
BLOCK = 256
INNER = 1536
CHANNELS = 1792
PROJ = 3352
RAW = 3765320
PARAMS = 3768320


norm_epsilon = 1e-05
beta_one = 0.9
beta_two = 0.999
learn_rate = 0.02
weight_decay = 0.01
adam_epsilon = 1e-08
adam_step = 2
highest = lax.Precision.HIGHEST


def passed_along(value, axis, by):
    length = lax.axis_size(axis)
    pairs = [(i, i + by) for i in range(length) if 0 <= i + by < length]
    return lax.ppermute(value, axis, pairs)

def silu_grad(pre_act):
    logistic = jax.nn.sigmoid(pre_act)
    return logistic * (1.0 + pre_act * (1.0 - logistic))


def adam_update(weights, gradient, first, second):
    first_new = beta_one * first + (1.0 - beta_one) * gradient
    second_new = beta_two * second + (1.0 - beta_two) * gradient * gradient
    corrected = first_new / (1.0 - beta_one**adam_step)
    scaled = jnp.sqrt(second_new / (1.0 - beta_two**adam_step))
    weights_new = weights - learn_rate * (
        corrected / (scaled + adam_epsilon) + weight_decay * weights
    )
    return (weights_new, first_new, second_new)


LANES = 128
PAIR = 2 * HEAD_DIM
f32 = jnp.float32
bf16 = jnp.bfloat16


def dot_ab(a, b):
    return lax.dot_general(a, b, (((1,), (0,)), ((), ())), preferred_element_type=f32)


def dot_abt(a, b):
    return lax.dot_general(a, b, (((1,), (1,)), ((), ())), preferred_element_type=f32)


def dot_atb(a, b):
    return lax.dot_general(a, b, (((0,), (0,)), ((), ())), preferred_element_type=f32)


def column_of(array, index):
    lane = lax.broadcasted_iota(jnp.int32, array.shape, 1)
    return jnp.sum(jnp.where(lane == index, array, 0.0), axis=1, keepdims=True)


def masked_scores(b_ref, c_ref):
    scores = dot_abt(c_ref[...], b_ref[...])
    row = lax.broadcasted_iota(jnp.int32, scores.shape, 0)
    col = lax.broadcasted_iota(jnp.int32, scores.shape, 1)
    return jnp.where(row >= col, scores, 0.0), row >= col


def inside_kernel(x_ref, b_ref, c_ref, cum_ref, cum_t_ref, dt_t_ref, y_ref, score_ref):
    score_ref[...], _ = masked_scores(b_ref, c_ref)

    def one(pair, carry):
        lanes = pl.ds(pl.multiple_of(pair * PAIR, PAIR), PAIR)
        block = x_ref[:, lanes]
        halves = []
        for side in range(2):
            head = 2 * pair + side
            spread = column_of(cum_ref[...], head) - cum_t_ref[pl.ds(head, 1), :]
            decay = jnp.exp(jnp.minimum(spread, 0.0))
            weights = score_ref[...] * decay * dt_t_ref[pl.ds(head, 1), :]
            halves.append(dot_ab(weights.astype(bf16), block))
        lane = lax.broadcasted_iota(jnp.int32, halves[0].shape, 1)
        y_ref[:, lanes] = jnp.where(lane < HEAD_DIM, halves[0], halves[1])
        return carry

    lax.fori_loop(0, MIXER_HEADS // 2, one, 0)


def inside_grad_kernel(
    x_ref, dy_ref, b_ref, c_ref, cum_ref, cum_t_ref, dt_t_ref,
    dx_ref, db_ref, dc_ref, rows_ref, cols_ref, score_ref, dscore_ref,
):
    score_ref[...], causal = masked_scores(b_ref, c_ref)
    dscore_ref[...] = jnp.zeros_like(dscore_ref)
    rows_ref[...] = jnp.zeros_like(rows_ref)
    row_lane = lax.broadcasted_iota(jnp.int32, rows_ref.shape, 1)

    def one(pair, carry):
        lanes = pl.ds(pl.multiple_of(pair * PAIR, PAIR), PAIR)
        block = x_ref[:, lanes]
        dy = dy_ref[:, lanes]
        lane = lax.broadcasted_iota(jnp.int32, dy.shape, 1)
        halves = []
        for side in range(2):
            head = 2 * pair + side
            mine = (lane < HEAD_DIM) if side == 0 else (lane >= HEAD_DIM)
            dy_head = jnp.where(mine, dy, jnp.zeros_like(dy))
            dt_row = dt_t_ref[pl.ds(head, 1), :]
            spread = column_of(cum_ref[...], head) - cum_t_ref[pl.ds(head, 1), :]
            decay = jnp.exp(jnp.minimum(spread, 0.0))
            scaled = score_ref[...] * decay
            d_weights = dot_abt(dy_head, block)
            halves.append(dot_atb((scaled * dt_row).astype(bf16), dy_head))
            dscore_ref[...] += d_weights * decay * dt_row
            mass = d_weights * scaled
            cols_ref[pl.ds(head, 1), :] = jnp.sum(mass, axis=0, keepdims=True)
            row_sum = jnp.sum(mass * dt_row, axis=1, keepdims=True)
            rows_ref[...] += jnp.where(row_lane == head, row_sum, 0.0)
        dx_ref[:, lanes] = halves[0] + halves[1]
        return carry

    lax.fori_loop(0, MIXER_HEADS // 2, one, 0)
    d_scores = jnp.where(causal, dscore_ref[...], 0.0).astype(bf16)
    dc_ref[...] = dot_ab(d_scores, b_ref[...])
    db_ref[...] = dot_atb(d_scores, c_ref[...])


def whole_vmem(count):
    return [pl.BlockSpec(memory_space=pltpu.VMEM)] * count


def inside_forward(x, b, c, cum, cum_t, dt_t):
    tokens = x.shape[0]
    return pl.pallas_call(
        inside_kernel,
        out_shape=jax.ShapeDtypeStruct((tokens, INNER), f32),
        in_specs=whole_vmem(6),
        out_specs=pl.BlockSpec(memory_space=pltpu.VMEM),
        scratch_shapes=[pltpu.VMEM((tokens, tokens), f32)],
        cost_estimate=pl.CostEstimate(
            flops=4 * tokens * tokens * INNER, bytes_accessed=4 * tokens * INNER,
            transcendentals=tokens * tokens * MIXER_HEADS,
        ),
        name="inside_forward",
    )(x, b, c, cum, cum_t, dt_t)


def inside_backward(x, dy, b, c, cum, cum_t, dt_t):
    tokens = x.shape[0]
    return pl.pallas_call(
        inside_grad_kernel,
        out_shape=(
            jax.ShapeDtypeStruct((tokens, INNER), f32),
            jax.ShapeDtypeStruct((tokens, STATE), f32),
            jax.ShapeDtypeStruct((tokens, STATE), f32),
            jax.ShapeDtypeStruct((tokens, LANES), f32),
            jax.ShapeDtypeStruct((MIXER_HEADS, tokens), f32),
        ),
        in_specs=whole_vmem(7),
        out_specs=tuple(whole_vmem(5)),
        scratch_shapes=[pltpu.VMEM((tokens, tokens), f32), pltpu.VMEM((tokens, tokens), f32)],
        cost_estimate=pl.CostEstimate(
            flops=8 * tokens * tokens * INNER, bytes_accessed=8 * tokens * INNER,
            transcendentals=tokens * tokens * MIXER_HEADS,
        ),
        name="inside_backward",
    )(x, dy, b, c, cum, cum_t, dt_t)


def row_major(array):
    return with_layout_constraint(array, Layout(major_to_minor=(0, 1)))


def head_map():
    owner = lax.broadcasted_iota(jnp.int32, (MIXER_HEADS, INNER), 1) // HEAD_DIM
    return (owner == lax.broadcasted_iota(jnp.int32, (MIXER_HEADS, INNER), 0)).astype(f32)


def per_channel(value):
    return jnp.dot(value, head_map(), precision=highest)


def per_head(value):
    return lax.dot_general(
        value, head_map(), (((1,), (1,)), ((), ())), precision=highest, preferred_element_type=f32
    )


def bit_plan():
    seq_bits = lax.axis_size("seq").bit_length() - 1
    fsdp_bits = lax.axis_size("fsdp").bit_length() - 1
    dims = [("seq", bit) for bit in reversed(range(seq_bits))]
    dims += [("fsdp", bit) for bit in reversed(range(fsdp_bits))]
    middle = [("seq", bit) for bit in range(1, seq_bits)]
    last = [("fsdp", bit) for bit in range(fsdp_bits)]
    orders = [
        [dims.index(step) for step in [("seq", 0)] + middle + last],
        [dims.index(step) for step in [("seq", 0)] + middle[::-1] + last],
    ]
    return dims, orders


def kernels_fit(rows):
    seq, fsdp = lax.axis_size("seq"), lax.axis_size("fsdp")
    return rows % 8 == 0 and rows >= 64 and seq > 1 and seq & (seq - 1) == 0 and fsdp & (fsdp - 1) == 0


def row_streams(rows, parts):
    tiles = rows // 16
    edges = [16 * (tiles * part // parts) for part in range(parts)] + [rows]
    return list(zip(edges[:-1], edges[1:]))


def my_bits(dims):
    index = {axis: lax.axis_index(axis) for axis in ("seq", "fsdp")}
    return [(index[axis] // (1 << bit)) % 2 for axis, bit in dims], index


def partner_of(dims, index, bits, dim):
    axis, bit = dims[dim]
    return {axis: index[axis] + (1 - 2 * bits[dim]) * (1 << bit)}


def greet(dims, index, bits):
    barrier = pltpu.get_barrier_semaphore()
    for dim in range(len(dims)):
        pl.semaphore_signal(
            barrier, inc=1, device_id=partner_of(dims, index, bits, dim),
            device_id_type=pl.DeviceIdType.MESH,
        )
    pl.semaphore_wait(barrier, len(dims))


def scatter_sum(parts, rows):
    dims, orders = bit_plan()
    depth = len(dims)
    streams = row_streams(rows, 6)
    blocks = lax.axis_size("seq") * lax.axis_size("fsdp")
    copies = []
    start = 0
    for which, part in enumerate(parts):
        row = 0
        while row < part.shape[0]:
            block, inner = divmod(start + row, rows)
            size = min(rows - inner, part.shape[0] - row)
            copies.append((which, row, block, inner, size))
            row += size
        start += part.shape[0]
    assert start == blocks * rows

    def kernel(*refs):
        sources = refs[: len(parts)]
        out_ref, work, local_sem, send_sem, recv_sem = refs[len(parts) : len(parts) + 5]
        landing = refs[len(parts) + 5 :]
        bits, index = my_bits(dims)
        local = []
        for at, (which, row, block, inner, size) in enumerate(copies):
            where = tuple((block >> (depth - 1 - dim)) % 2 for dim in range(depth))
            copy = pltpu.make_async_copy(
                sources[which].at[pl.ds(row, size)],
                work.at[where + (pl.ds(inner, size),)],
                local_sem.at[at],
            )
            copy.start()
            local.append(copy)
        greet(dims, index, bits)
        for copy in local:
            copy.wait()
        sent = []

        def region(stream, stage, flip):
            first, last = streams[stream]
            order = orders[stream % 2]
            where = [slice(None)] * depth
            for dim in order[:stage]:
                where[dim] = bits[dim]
            where[order[stage]] = 1 - bits[order[stage]] if flip else bits[order[stage]]
            return where, pl.ds(first, last - first)

        def take(stream, stage):
            sent[stage * len(streams) + stream].wait_recv()
            arrived = landing[stage * len(streams) + stream]
            where, lines = region(stream, stage, False)
            free = [dim for dim in range(depth) if isinstance(where[dim], slice)]
            for choice in itertools.product(range(2), repeat=len(free)):
                spot = list(where)
                for dim, value in zip(free, choice):
                    spot[dim] = value
                total = work[tuple(spot) + (lines,)].astype(f32) + arrived[choice].astype(f32)
                if stage == depth - 1:
                    out_ref[lines] = total.astype(bf16)
                else:
                    work[tuple(spot) + (lines,)] = total.astype(bf16)

        for stage in range(depth):
            for stream in range(len(streams)):
                if stage > 0:
                    take(stream, stage - 1)
                where, lines = region(stream, stage, True)
                slot = stage * len(streams) + stream
                copy = pltpu.make_async_remote_copy(
                    src_ref=work.at[tuple(where) + (lines,)],
                    dst_ref=landing[slot],
                    send_sem=send_sem.at[slot],
                    recv_sem=recv_sem.at[slot],
                    device_id=partner_of(dims, index, bits, orders[stream % 2][stage]),
                    device_id_type=pl.DeviceIdType.MESH,
                )
                copy.start()
                sent.append(copy)
        for stream in range(len(streams)):
            take(stream, depth - 1)
        for copy in sent:
            copy.wait_send()

    slots = depth * len(streams)
    buffers = [
        pltpu.VMEM((2,) * (depth - 1 - stage) + (last - first, LANES), bf16)
        for stage in range(depth)
        for first, last in streams
    ]
    return pl.pallas_call(
        kernel,
        out_shape=jax.ShapeDtypeStruct((rows, LANES), bf16),
        in_specs=[pl.BlockSpec(memory_space=pl.ANY)] * len(parts),
        out_specs=pl.BlockSpec(memory_space=pltpu.VMEM),
        scratch_shapes=[
            pltpu.VMEM((2,) * depth + (rows, LANES), bf16),
            pltpu.SemaphoreType.DMA((len(copies),)),
            pltpu.SemaphoreType.DMA((slots,)),
            pltpu.SemaphoreType.DMA((slots,)),
        ] + buffers,
        compiler_params=pltpu.CompilerParams(
            collective_id=0, has_side_effects=True, vmem_limit_bytes=40 * 2**20
        ),
        name="scatter_sum",
    )(*parts)


def gather_all(shard):
    dims, orders = bit_plan()
    orders = [order[::-1] for order in orders]
    depth = len(dims)
    rows = shard.shape[0]
    streams = row_streams(rows, 8)

    def kernel(shard_ref, out_ref, local_sem, send_sem, recv_sem):
        bits, index = my_bits(dims)
        own = pltpu.make_async_copy(shard_ref, out_ref.at[tuple(bits)], local_sem)
        own.start()
        greet(dims, index, bits)
        own.wait()
        sent = []
        for stage in range(depth):
            for stream, (first, last) in enumerate(streams):
                order = orders[stream % 2]
                if stage > 0:
                    sent[(stage - 1) * len(streams) + stream].wait_recv()
                where = list(bits)
                for dim in order[:stage]:
                    where[dim] = slice(None)
                area = out_ref.at[tuple(where) + (pl.ds(first, last - first),)]
                slot = stage * len(streams) + stream
                copy = pltpu.make_async_remote_copy(
                    src_ref=area,
                    dst_ref=area,
                    send_sem=send_sem.at[slot],
                    recv_sem=recv_sem.at[slot],
                    device_id=partner_of(dims, index, bits, order[stage]),
                    device_id_type=pl.DeviceIdType.MESH,
                )
                copy.start()
                sent.append(copy)
        for copy in sent[-len(streams) :]:
            copy.wait_recv()
        for copy in sent:
            copy.wait_send()

    slots = depth * len(streams)
    whole = pl.pallas_call(
        kernel,
        out_shape=jax.ShapeDtypeStruct((2,) * depth + (rows, LANES), bf16),
        in_specs=[pl.BlockSpec(memory_space=pltpu.VMEM)],
        out_specs=pl.BlockSpec(memory_space=pl.ANY),
        scratch_shapes=[
            pltpu.SemaphoreType.DMA,
            pltpu.SemaphoreType.DMA((slots,)),
            pltpu.SemaphoreType.DMA((slots,)),
        ],
        compiler_params=pltpu.CompilerParams(collective_id=1, has_side_effects=True),
        name="gather_all",
    )(shard)
    return whole.reshape(-1, LANES)


def body(block_input, out_grad, params, first_moment, second_moment):
    shard_half = params.astype(bf16).reshape(-1, LANES)
    if kernels_fit(shard_half.shape[0]):
        whole_half = gather_all(shard_half)
    else:
        whole_half = lax.all_gather(shard_half, ("seq", "fsdp"), axis=0, tiled=True)
    sizes = [MODEL_WIDTH * PROJ, INNER * MODEL_WIDTH, KERNEL * CHANNELS, CHANNELS, MODEL_WIDTH, INNER]
    pieces = []
    row = 0
    for size in sizes:
        pieces.append(whole_half[row : row + size // LANES])
        row = row + size // LANES
    in_weight = pieces[0].reshape(MODEL_WIDTH, PROJ)
    out_weight = pieces[1].reshape(INNER, MODEL_WIDTH)
    conv_weight = pieces[2].astype(f32).reshape(KERNEL, CHANNELS)
    conv_bias = pieces[3].astype(f32).reshape(-1)
    gain_input = pieces[4].astype(f32).reshape(-1)
    gain_gated = pieces[5].astype(f32).reshape(-1)
    small = whole_half[row : row + 1].astype(f32).reshape(-1)
    dt_bias = small[:MIXER_HEADS]
    a_log = small[MIXER_HEADS : 2 * MIXER_HEADS]
    skip_gain = small[2 * MIXER_HEADS : 3 * MIXER_HEADS]
    residual = block_input[0].astype(f32)
    cotangent = out_grad[0]
    tokens_dev = residual.shape[0]
    inv_rms = lax.rsqrt(jnp.mean(residual * residual, axis=-1, keepdims=True) + norm_epsilon)
    normed = (residual * inv_rms * gain_input).astype(bf16)
    projected = row_major(jnp.dot(normed, in_weight, preferred_element_type=f32).astype(bf16))
    gate_z = projected[:, :INNER].astype(f32)
    conv_in = projected[:, INNER : INNER + CHANNELS]
    dt_raw = projected[:, INNER + CHANNELS :].astype(f32)
    left_rows = passed_along(conv_in[tokens_dev - KERNEL + 1 :], "seq", 1)
    padded = jnp.concatenate([left_rows, conv_in], 0).astype(f32)
    conv_out = jnp.zeros((tokens_dev, CHANNELS), f32) + conv_bias[None, :]
    for tap_index in range(KERNEL):
        conv_out = (
            conv_out + conv_weight[tap_index][None, :] * padded[tap_index : tap_index + tokens_dev]
        )
    activated = row_major(jax.nn.silu(conv_out).astype(bf16))
    x_half = activated[:, :INNER]
    b_half = activated[:, INNER : INNER + STATE]
    c_half = activated[:, INNER + STATE :]
    values = x_half.astype(f32)
    pre_dt = dt_raw + dt_bias[None, :]
    steps_dt = jax.nn.softplus(pre_dt)
    a_rate = -jnp.exp(a_log)
    log_decay = steps_dt * a_rate[None, :]
    causal = jnp.arange(tokens_dev)[:, None] >= jnp.arange(tokens_dev)[None, :]
    triangle = causal.astype(f32)
    cumulative = jnp.dot(triangle, log_decay, precision=highest)
    segment_log = cumulative[-1]
    cum_t, dt_t = cumulative.T, steps_dt.T
    cum_wide = jnp.pad(cumulative, ((0, 0), (0, LANES - MIXER_HEADS)))
    to_end = jnp.exp(segment_log[None, :] - cumulative)
    from_start = jnp.exp(cumulative)
    tail_weight = per_channel(to_end * steps_dt)
    head_weight = per_channel(from_start)
    x_tail = (values * tail_weight).astype(bf16)
    local_state = dot_atb(x_tail, b_half).astype(bf16)
    log_high = lax.reduce_precision(segment_log, 8, 7)
    log_rows = jnp.concatenate(
        [log_high, segment_log - log_high, jnp.zeros((LANES - 2 * MIXER_HEADS,), f32)]
    )
    log_rows = jnp.pad(log_rows[None, :], ((0, 15), (0, 0))).astype(bf16)
    count, mine = lax.axis_size("seq"), lax.axis_index("seq")
    gathered = lax.all_gather(jnp.concatenate([local_state, log_rows], 0), "seq")
    y_inside = inside_forward(x_half, b_half, c_half, cum_wide, cum_t, dt_t)
    logs = gathered[:, INNER].astype(f32)
    logs = logs[:, :MIXER_HEADS] + logs[:, MIXER_HEADS : 2 * MIXER_HEADS]
    source = jnp.arange(count)
    between = (source[None, :] > source[:, None]) & (source[None, :] < mine)
    earlier = jnp.exp(jnp.sum(jnp.where(between[:, :, None], logs[None], 0.0), 1))
    earlier = per_channel(jnp.where(source[:, None] < mine, earlier, 0.0))
    between = (source[None, :] < source[:, None]) & (source[None, :] > mine)
    later = jnp.exp(jnp.sum(jnp.where(between[:, :, None], logs[None], 0.0), 1))
    later = per_channel(jnp.where(source[:, None] > mine, later, 0.0))
    state_in = jnp.sum(gathered[:, :INNER].astype(f32) * earlier[:, :, None], 0)
    state_half = state_in.astype(bf16)
    y_carried = dot_abt(c_half, state_half) * head_weight
    skip_wide = per_channel(skip_gain[None, :])
    y_carried = row_major(y_carried)
    mixed = y_inside + y_carried + skip_wide * values
    gate_act = jax.nn.silu(gate_z)
    gated = mixed * gate_act
    inv_gated = lax.rsqrt(jnp.mean(gated * gated, axis=-1, keepdims=True) + norm_epsilon)
    normed_out = (gated * inv_gated * gain_gated).astype(bf16)
    output = residual + jnp.dot(normed_out, out_weight, preferred_element_type=f32)
    d_out_weight = dot_atb(normed_out, cotangent).astype(bf16)
    d_normed_out = row_major(dot_abt(cotangent, out_weight))
    d_gain_gated = jnp.sum(d_normed_out * gated * inv_gated, 0)
    scaled_grad = d_normed_out * gain_gated
    d_gated = inv_gated * scaled_grad - gated * inv_gated**3 * jnp.mean(
        scaled_grad * gated, axis=-1, keepdims=True
    )
    d_mixed = d_gated * gate_act
    d_gate_z = d_gated * mixed * silu_grad(gate_z)
    d_skip = per_head(jnp.sum(d_mixed * values, 0)[None, :])[0]
    dy_half = row_major(d_mixed.astype(bf16))
    dy_head = (d_mixed * head_weight).astype(bf16)
    local_grad = dot_atb(dy_head, c_half).astype(bf16)
    gathered_grad = lax.all_gather(local_grad, "seq")
    dx_inside, db_inside, dc_inside, row_mass, col_mass = inside_backward(
        x_half, dy_half, b_half, c_half, cum_wide, cum_t, dt_t
    )
    later_grad = jnp.sum(gathered_grad.astype(f32) * later[:, :, None], 0)
    grad_half = later_grad.astype(bf16)
    bg = row_major(dot_abt(b_half, grad_half))
    d_values = dx_inside + tail_weight * bg + skip_wide * d_mixed
    d_inputs_b = db_inside + dot_ab(x_tail, grad_half)
    d_outputs_c = dc_inside + dot_ab(dy_head, state_half)
    tail_mass = per_head(values * bg) * to_end
    d_steps_ssd = col_mass.T + tail_mass
    state_mass = per_head(jnp.sum(later_grad * state_in, 1)[None, :])[0]
    d_cumulative = row_mass[:, :MIXER_HEADS] + per_head(d_mixed * y_carried) - steps_dt * d_steps_ssd
    d_last = jnp.sum(steps_dt * tail_mass, 0) + jnp.exp(segment_log) * state_mass
    d_log_decay = d_last[None, :] + lax.dot_general(
        triangle, d_cumulative, (((0,), (0,)), ((), ())), precision=highest
    )
    d_steps = d_steps_ssd + d_log_decay * a_rate[None, :]
    d_a_log = jnp.sum(d_log_decay * steps_dt, 0) * a_rate
    d_pre_dt = d_steps * jax.nn.sigmoid(pre_dt)
    d_dt_bias = jnp.sum(d_pre_dt, 0)
    d_activated = jnp.concatenate([d_values, d_inputs_b, d_outputs_c], 1)
    d_conv_out = row_major(d_activated * silu_grad(conv_out))
    d_conv_bias = jnp.sum(d_conv_out, 0)
    d_conv_weight = jnp.stack(
        [
            jnp.sum(d_conv_out * padded[tap_index : tap_index + tokens_dev], 0)
            for tap_index in range(KERNEL)
        ],
        0,
    )
    d_padded = jnp.zeros((tokens_dev + KERNEL - 1, CHANNELS), jnp.float32)
    for tap_index in range(KERNEL):
        d_padded = d_padded + jnp.pad(
            d_conv_out * conv_weight[tap_index][None, :],
            ((tap_index, KERNEL - 1 - tap_index), (0, 0)),
        )
    right_rows = passed_along(d_padded[: KERNEL - 1], "seq", -1)
    d_conv_in = d_padded[KERNEL - 1 :]
    d_conv_in = jnp.concatenate(
        [d_conv_in[: tokens_dev - KERNEL + 1], d_conv_in[tokens_dev - KERNEL + 1 :] + right_rows], 0
    )
    d_projected = row_major(jnp.concatenate([d_gate_z, d_conv_in, d_pre_dt], 1).astype(bf16))
    d_in_weight = row_major(dot_atb(normed, d_projected).astype(bf16))
    d_normed = jnp.dot(d_projected, in_weight.T, preferred_element_type=jnp.float32)
    d_gain_input = jnp.sum(d_normed * residual * inv_rms, 0)
    scaled_in = d_normed * gain_input
    d_residual = inv_rms * scaled_in - residual * inv_rms**3 * jnp.mean(
        scaled_in * residual, axis=-1, keepdims=True
    )
    input_grad = cotangent.astype(jnp.float32) + d_residual
    tail_vector = jnp.concatenate(
        [d_dt_bias, d_a_log, d_skip, jnp.zeros((PARAMS - RAW,), f32)]
    )
    small_parts = [d_conv_weight, d_conv_bias, d_gain_input, d_gain_gated, tail_vector]
    small_rows = jnp.concatenate([part.astype(bf16).reshape(-1, LANES) for part in small_parts], 0)
    parts = [d_in_weight.astype(bf16).reshape(-1, LANES), d_out_weight.reshape(-1, LANES), small_rows]
    if kernels_fit(shard_half.shape[0]):
        grad_shard = scatter_sum(parts, shard_half.shape[0])
    else:
        flat_local = jnp.concatenate(parts, 0)
        grad_shard = lax.psum_scatter(flat_local, ("seq", "fsdp"), scatter_dimension=0, tiled=True)
    grad_shard = grad_shard.reshape(-1).astype(f32)
    new_params, new_first, new_second = adam_update(params, grad_shard, first_moment, second_moment)
    return (output[None], input_grad[None], grad_shard, new_params, new_first, new_second)


def solution(mesh):
    return jax.shard_map(
        body,
        mesh=mesh,
        in_specs=(
            P("fsdp", "seq", None),
            P("fsdp", "seq", None),
            P(("seq", "fsdp")),
            P(("seq", "fsdp")),
            P(("seq", "fsdp")),
        ),
        out_specs=(
            P("fsdp", "seq", None),
            P("fsdp", "seq", None),
            P(("seq", "fsdp")),
            P(("seq", "fsdp")),
            P(("seq", "fsdp")),
            P(("seq", "fsdp")),
        ),
        check_vma=False,
    )
```
